32 devices in a mesh: grp: 2 (over y), chan: 4 (over z), freq: 2 (over x), section: 2 (over core).
Axes of the slice: x: 2, y: 2, z: 4, core: 2. Of those that a mesh axis runs over, the one named last changes fastest.
Arguments:
- traces: bfloat16 [1024, 128, 384], P(('grp', 'chan'), ('freq', 'section')), parts along dimension 0, may hold values from -6 to 6
- offsets: int32 [256], P(('grp', 'freq', 'section')), parts along dimension 0, may hold values from 0 to 64
- freq_bins: int32 [128], replicated, may hold values from 0 to 128, as said below
- channel_alive: int32 [1024], P(('grp', 'chan')), parts along dimension 0, may hold values 0 or 1
Outputs:
- cross_spectra: bfloat16 [2, 128, 1024, 512], P(None, ('freq', 'section'), ('grp', 'chan')), parts along dimension 2
The draws below stay inside these ranges and needn't reach their ends.
There are 2 independent parts, one for each index of `grp`. The reference program is written for one: setup_inputs(seed, part) draws one part's arguments, and reference() takes and returns one part's arrays. A program takes and returns all parts, laid end to end along the dimension named above; an argument that names none is the same for every part. Nothing has to cross between parts.
Inputs may be any that keep to these rules, and one draw needn't show every extreme that they name: `freq_bins`: distinct and increasing.
All inputs are finite; a program needn't handle non-finite values. No bound on the sum of `channel_alive` on one device may be relied on, other than what follows from the above.
Results may differ from the reference program's by a relative error of at most 0.0025.
The reference program's roundings to bfloat16 on the way (of `fir_matrix`, `normed`, `table`, `spectra` and `whitened`) count: a program that leaves them out, or rounds other values in their place, can miss the bound.
Values may be sent and summed in bfloat16 or wider, within the bound.
A program may use at most 128 MiB of HBM per device.

```python
import math
import jax
import jax.numpy as jnp
from jax import lax

CB = 128
L = 256
BINS = 128
TAPS = 64
MAXOFF = 64
HALF = 64
SEG = 384
CH = 512
WINDOWS = 128
SPAN = 512


def draw_offsets(key, part):
    values = jax.random.randint(key, (WINDOWS,), 0, MAXOFF + 1, dtype=jnp.int32)
    return values.at[0].set(MAXOFF).at[WINDOWS - 1].set(0)


def draw_freq_bins(key, part):
    middle = jax.random.permutation(key, L // 2 - 1)[:BINS - 2].astype(jnp.int32) + 1
    chosen = jnp.concatenate([jnp.zeros((1,), jnp.int32), middle, jnp.full((1,), L // 2, jnp.int32)])
    return jnp.sort(chosen)


def with_ends(values, rng, least, largest):
    longest = values.shape.index(max(values.shape))
    spots = []
    for shift in (0, 1):
        where = [jax.random.randint(jax.random.fold_in(rng, axis), (), 0, length) for axis, length in enumerate(values.shape)]
        where[longest] = (where[longest] + shift) % values.shape[longest]
        spots.append(tuple(where))
    return values.at[spots[0]].set(least).at[spots[1]].set(largest)


def shard_levels(rng, extent, shards, low, top_value):
    def one(dim, parts):
        steps = jax.random.uniform(jax.random.fold_in(jax.random.fold_in(rng, 6), dim), (parts,), jnp.float32, low / len(shards), top_value / len(shards))
        return jnp.repeat(jnp.exp(steps), extent[dim] // parts).reshape((-1,) + (1,) * (len(extent) - dim - 1))

    level = one(*shards[0])
    for cut in shards[1:]:
        level = level * one(*cut)
    return level


def scatter_about(stream_key, extent, deviation, most, pieces=(), kind=jnp.bfloat16):
    result = jax.random.normal(stream_key, extent, jnp.float32) * deviation
    if len(pieces) > 0:
        result = shard_levels(stream_key, extent, pieces, -0.22, 0.18) * result
    return jnp.clip(result, min=-most, max=most).astype(kind)


def setup_inputs(seed: int = 0, part: int = 0) -> dict:
    splits = jax.random.split(jax.random.key(seed), 5)
    own_keys = jax.random.split(jax.random.fold_in(splits[4], part), 5)
    traces = scatter_about(own_keys[0], (CH, WINDOWS, SEG), 1.0, 6.0, ((0, 4), (1, 4)))
    offsets = draw_offsets(jax.random.fold_in(jax.random.fold_in(splits[4], part), 71), part)
    freq_bins = draw_freq_bins(jax.random.fold_in(splits[4], 71), part)
    channel_alive = with_ends((jax.random.randint(own_keys[3], (CH,), 0, 16) < 15).astype(jnp.int32), jax.random.fold_in(own_keys[3], 1), 0, 1)
    return {"traces": traces, "offsets": offsets, "freq_bins": freq_bins, "channel_alive": channel_alive}


eps_time = 1e-05
eps_power = 1e-06
low_cut = 0.04
high_cut = 0.42

def filter_matrix(offsets, seg_len, length, tap_count):
    sample = jnp.arange(seg_len, dtype=jnp.int32)[None, :, None]
    out_pos = jnp.arange(length, dtype=jnp.int32)[None, None, :]
    lag_steps = sample - offsets.astype(jnp.int32)[:, None, None] - out_pos
    lag_value = lag_steps.astype(jnp.float32)
    centre = lag_value - (tap_count - 1) / 2.0
    hann_taper = 0.5 - 0.5 * jnp.cos(2.0 * math.pi * lag_value / (tap_count - 1))
    band_pass = 2.0 * high_cut * jnp.sinc(2.0 * high_cut * centre) - 2.0 * low_cut * jnp.sinc(2.0 * low_cut * centre)
    inside = (lag_steps >= 0) & (lag_steps < tap_count)
    return jnp.where(inside, hann_taper * band_pass, jnp.float32(0.0)).astype(jnp.bfloat16)

def mean_matrix(length, half_width):
    first = jnp.arange(length, dtype=jnp.int32)[:, None]
    second = jnp.arange(length, dtype=jnp.int32)[None, :]
    nearby = (jnp.abs(first - second) <= half_width).astype(jnp.float32)
    return nearby / lax.optimization_barrier(jnp.sum(nearby, axis=0, keepdims=True))

def dft_table(freq_bins, length):
    positions = jnp.arange(length, dtype=jnp.int32)[:, None]
    angles = (positions * freq_bins.astype(jnp.int32)[None, :] % length).astype(jnp.float32) * (2.0 * math.pi / length)
    return jnp.concatenate([jnp.cos(angles), -jnp.sin(angles)], axis=1).astype(jnp.bfloat16)

def whiten(halves, alive):
    values = halves.astype(jnp.float32)
    bin_power = lax.optimization_barrier(jnp.mean(values[0] * values[0] + values[1] * values[1], axis=1))
    weights = lax.rsqrt(bin_power + eps_power) * alive.astype(jnp.float32)[None, :]
    scaled = values * weights[None, :, None, :]
    return jnp.transpose(scaled, (1, 3, 0, 2)).reshape(halves.shape[1], halves.shape[3], -1).astype(jnp.bfloat16)

def reference(traces, offsets, freq_bins, channel_alive):
    fir_matrix = filter_matrix(offsets, SEG, L, TAPS).astype(jnp.float32)
    band_mean = mean_matrix(L, HALF)
    table = dft_table(freq_bins, L).astype(jnp.float32)
    blocks = traces.reshape(CH // CB, CB, WINDOWS, SEG)
    alive_blocks = channel_alive.reshape(CH // CB, CB)

    def prepare(pair):
        block_traces, alive = pair
        filtered = jnp.einsum('cws,wsn->wcn', block_traces.astype(jnp.float32), fir_matrix)
        rows = filtered.reshape(-1, L)
        envelope = jnp.dot(jnp.abs(rows), band_mean, precision=lax.Precision.HIGHEST, preferred_element_type=jnp.float32)
        normed = (rows / (envelope + eps_time)).reshape(filtered.shape).astype(jnp.bfloat16)
        spectra = jnp.einsum('wcn,nj->jwc', normed.astype(jnp.float32), table).astype(jnp.bfloat16)
        return whiten(spectra.reshape(2, BINS, WINDOWS, CB), alive)
    whitened = lax.map(prepare, (blocks, alive_blocks))
    whitened = jnp.transpose(whitened, (1, 0, 2, 3)).reshape(BINS, CH // SPAN, SPAN, 2 * WINDOWS)

    def correlate(slab):
        real_part = slab[..., :WINDOWS]
        imag_part = slab[..., WINDOWS:]
        left_side = jnp.stack([slab, jnp.concatenate([imag_part, -real_part], axis=-1)])
        product = jnp.einsum('poik,ojk->poij', left_side.astype(jnp.float32), slab.astype(jnp.float32))
        return (product * (1.0 / WINDOWS)).astype(jnp.bfloat16).reshape(2, CH, SPAN)
    cross = lax.map(correlate, whitened)
    return jnp.transpose(cross, (1, 0, 2, 3))
```

```python
import functools
import math

import jax
import jax.numpy as jnp
from jax import lax
from jax.experimental import pallas as pl
from jax.experimental.pallas import tpu as pltpu
from jax.sharding import PartitionSpec as P

L = 256
BINS = 128
TAPS = 64
HALF = 64
MAXOFF = 64

eps_time = 1e-05
eps_power = 1e-06
low_cut = 0.04
high_cut = 0.42

MESH = pl.DeviceIdType.MESH
F32 = jnp.float32
BF16 = jnp.bfloat16


def toeplitz(length, depth, tap_count):
    out_pos = jnp.arange(length, dtype=jnp.int32)[:, None]
    sample = jnp.arange(depth, dtype=jnp.int32)[None, :]
    lag_steps = sample - out_pos
    lag_value = lag_steps.astype(F32)
    centre = lag_value - (tap_count - 1) / 2.0
    hann_taper = 0.5 - 0.5 * jnp.cos(2.0 * math.pi * lag_value / (tap_count - 1))
    band_pass = 2.0 * high_cut * jnp.sinc(2.0 * high_cut * centre) - 2.0 * low_cut * jnp.sinc(
        2.0 * low_cut * centre
    )
    inside = (lag_steps >= 0) & (lag_steps < tap_count)
    return jnp.where(inside, hann_taper * band_pass, F32(0.0)).astype(BF16)


def dft_rows(freq_bins, length, owners):
    positions = jnp.arange(length, dtype=jnp.int32)[None, :]
    angles = (positions * freq_bins[:, None] % length).astype(F32) * (2.0 * math.pi / length)
    table = jnp.stack([jnp.cos(angles), -jnp.sin(angles)]).astype(BF16)
    table = table.reshape(2, owners, -1, length)
    return jnp.swapaxes(table, 0, 1).reshape(-1, length)


def spectra_kernel(offsets, x_ref, fir_ref, table_ref, alive_ref, out_ref, seg, acc):
    step = pl.program_id(0)
    batch, _, chans = x_ref.shape
    depth = fir_ref.shape[1]
    rows, wins = table_ref.shape[0], out_ref.shape[0] // table_ref.shape[0]
    shifted = []
    for i in range(batch):
        seg[i] = x_ref[i].astype(F32)
        shifted.append(seg[i, pl.ds(offsets[step * batch + i], depth), :].astype(BF16))
    filtered = jnp.dot(fir_ref[...], jnp.concatenate(shifted, axis=1), preferred_element_type=F32)
    first = lax.broadcasted_iota(jnp.int32, (L, L), 0)
    second = lax.broadcasted_iota(jnp.int32, (L, L), 1)
    band = jnp.where(jnp.abs(first - second) <= HALF, F32(1), F32(0)).astype(BF16)
    size = jnp.abs(filtered)
    high = size.astype(BF16)
    rest = size - high.astype(F32)
    mid = rest.astype(BF16)
    low = (rest - mid.astype(F32)).astype(BF16)
    total = jnp.dot(band, high, preferred_element_type=F32)
    total += jnp.dot(band, mid, preferred_element_type=F32)
    total += jnp.dot(band, low, preferred_element_type=F32)
    place = lax.broadcasted_iota(jnp.int32, (L, 1), 0)
    count = jnp.minimum(place + HALF, L - 1) - jnp.maximum(place - HALF, 0) + 1
    envelope = total * (1.0 / count.astype(F32))
    normed = (filtered / (envelope + eps_time)).astype(BF16)
    spectra = jnp.dot(table_ref[...], normed, preferred_element_type=F32)
    alive = alive_ref[...].astype(F32)
    for i in range(batch):
        acc[pl.ds(step * batch + i, rows, stride=wins), :] = (
            spectra[:, i * chans : (i + 1) * chans] * alive
        )

    @pl.when(step == pl.num_programs(0) - 1)
    def _():
        out_ref[...] = acc[...].astype(BF16)


def gather_kernel(owners, sections, group, spec, gath, put_sem, a2a_send, a2a_recv, up_send, up_recv, dn_send, dn_recv):
    chan = lax.axis_index("chan")
    place = lax.rem(chan, group)
    mine = lax.axis_index("freq") * sections + lax.axis_index("section")

    def other(d):
        q = mine
        for bit in range(d.bit_length()):
            if d >> bit & 1:
                q = q + (1 << bit) - 2 * (1 << bit) * lax.rem(mine // (1 << bit), 2)
        return q

    def peer(d):
        q = other(d)
        return {"freq": q // sections, "section": lax.rem(q, sections)}

    has_up, has_dn = place + 1 < group, place >= 1
    barrier = pltpu.get_barrier_semaphore()
    for d in range(1, owners):
        pl.semaphore_signal(barrier, inc=1, device_id=peer(d), device_id_type=MESH)

    @pl.when(has_up)
    def _():
        pl.semaphore_signal(barrier, inc=1, device_id={"chan": chan + 1}, device_id_type=MESH)

    @pl.when(has_dn)
    def _():
        pl.semaphore_signal(barrier, inc=1, device_id={"chan": chan - 1}, device_id_type=MESH)

    pl.semaphore_wait(barrier, owners - 1 + has_up.astype(jnp.int32) + has_dn.astype(jnp.int32))

    def a2a(d):
        return pltpu.make_async_remote_copy(
            src_ref=spec.at[other(d)],
            dst_ref=gath.at[place, mine],
            send_sem=a2a_send.at[d],
            recv_sem=a2a_recv.at[d],
            device_id=peer(d),
            device_id_type=MESH,
        )

    def hop(k, d, up):
        block = place - k if up else place + k
        source = spec.at[mine] if k == 0 and d == 0 else gath.at[block, other(d)]
        return pltpu.make_async_remote_copy(
            src_ref=source,
            dst_ref=gath.at[block, other(d)],
            send_sem=(up_send if up else dn_send).at[k, d],
            recv_sem=(up_recv if up else dn_recv).at[k, d],
            device_id={"chan": chan + 1 if up else chan - 1},
            device_id_type=MESH,
        )

    def send(k, d, finish=False):
        for up in (True, False):
            there = (place - k >= 0) & has_up if up else (place + k < group) & has_dn

            @pl.when(there)
            def _():
                copy = hop(k, d, up)
                if finish:
                    copy.wait_send()
                else:
                    copy.start()

    put = pltpu.make_async_copy(spec.at[mine], gath.at[place, mine], put_sem)
    send(0, 0)
    for d in range(1, owners):
        a2a(d).start()
    put.start()
    for d in range(1, owners):
        a2a(d).wait_recv()
        send(0, d)
    for k in range(1, group):
        for d in range(owners):
            for up in (True, False):
                comes = place - k >= 0 if up else place + k < group
                goes = has_up if up else has_dn

                @pl.when(comes)
                def _():
                    pltpu.make_async_remote_copy(
                        src_ref=spec.at[mine],
                        dst_ref=gath.at[place - k if up else place + k, other(d)],
                        send_sem=(up_send if up else dn_send).at[k - 1, d],
                        recv_sem=(up_recv if up else dn_recv).at[k - 1, d],
                        device_id={"chan": chan - 1 if up else chan + 1},
                        device_id_type=MESH,
                    ).wait_recv()

                @pl.when(comes & goes)
                def _():
                    hop(k, d, up).start()

    put.wait()
    for d in range(1, owners):
        a2a(d).wait_send()
    for k in range(group - 1):
        for d in range(owners):
            send(k, d, finish=True)


def cross_kernel(place, windows, data, out):
    group, owners, _, batch, wins, chans = data.shape
    mine = place[0]
    for f in range(batch):
        def whitened(b):
            values = data[b, :, :, f].astype(F32)
            values = jnp.swapaxes(values, 0, 1).reshape(2 * owners * wins, chans)
            power = jnp.sum(values * values, axis=0, keepdims=True) * (1.0 / windows)
            return (values * lax.rsqrt(power + eps_power)).astype(BF16)

        right = jnp.concatenate([whitened(b) for b in range(group)], axis=1)
        own = whitened(mine)
        half = owners * wins
        turned = jnp.concatenate([own[half:], -own[:half]], axis=0)
        left = jnp.concatenate([own, turned], axis=1)
        product = lax.dot_general(
            left, right, (((0,), (0,)), ((), ())), preferred_element_type=F32
        )
        scaled = (product * (1.0 / windows)).astype(BF16)
        out[0, f] = scaled[:chans]
        out[1, f] = scaled[chans:]


def local(sizes, traces, offsets, freq_bins, channel_alive):
    chans, wins, seg_len = traces.shape
    owners = sizes["freq"] * sizes["section"]
    group = min(8, sizes["chan"])
    bins = BINS // owners
    rows = 2 * bins * wins
    depth = seg_len - MAXOFF
    batch = 4
    whole = lambda *shape: pl.BlockSpec(shape, lambda *_: (0,) * len(shape))
    spectra = pl.pallas_call(
        spectra_kernel,
        grid_spec=pltpu.PrefetchScalarGridSpec(
            num_scalar_prefetch=1,
            grid=(wins // batch,),
            in_specs=[
                pl.BlockSpec((batch, seg_len, chans), lambda i, _: (i, 0, 0)),
                whole(L, depth),
                whole(2 * BINS, L),
                whole(1, chans),
            ],
            out_specs=whole(2 * BINS * wins, chans),
            scratch_shapes=[
                pltpu.VMEM((batch, seg_len, chans), F32),
                pltpu.VMEM((2 * BINS * wins, chans), F32),
            ],
        ),
        out_shape=jax.ShapeDtypeStruct((2 * BINS * wins, chans), BF16),
        name="spectra",
    )(
        offsets,
        jnp.transpose(traces, (1, 2, 0)),
        toeplitz(L, depth, TAPS),
        dft_rows(freq_bins, L, owners),
        channel_alive.reshape(1, chans),
    )
    dma = pltpu.SemaphoreType.DMA
    gathered = pl.pallas_call(
        functools.partial(gather_kernel, owners, sizes["section"], group),
        in_specs=[pl.BlockSpec(memory_space=pl.ANY)],
        out_specs=pl.BlockSpec(memory_space=pl.ANY),
        out_shape=jax.ShapeDtypeStruct((group, owners, rows, chans), BF16),
        scratch_shapes=[dma, dma((owners,)), dma((owners,))] + [dma((group, owners))] * 4,
        compiler_params=pltpu.CompilerParams(collective_id=0, has_side_effects=True),
        name="gather",
    )(spectra.reshape(owners, rows, chans))
    fold = 2
    place = lax.rem(lax.axis_index("chan"), group).astype(jnp.int32).reshape(1)
    return pl.pallas_call(
        lambda place, data, out: cross_kernel(place, wins * owners, data, out),
        grid_spec=pltpu.PrefetchScalarGridSpec(
            num_scalar_prefetch=1,
            grid=(bins // fold,),
            in_specs=[
                pl.BlockSpec(
                    (group, owners, 2, fold, wins, chans), lambda i, _: (0, 0, 0, i, 0, 0)
                )
            ],
            out_specs=pl.BlockSpec((2, fold, chans, group * chans), lambda i, _: (0, i, 0, 0)),
        ),
        out_shape=jax.ShapeDtypeStruct((2, bins, chans, group * chans), BF16),
        name="cross",
    )(place, gathered.reshape(group, owners, 2, bins, wins, chans))


def solution(mesh):
    in_specs = (
        P(("grp", "chan"), ("freq", "section"), None),
        P(("grp", "freq", "section")),
        P(),
        P(("grp", "chan")),
    )
    out_specs = P(None, ("freq", "section"), ("grp", "chan"), None)
    sizes = dict(mesh.shape)
    return jax.shard_map(
        functools.partial(local, sizes),
        mesh=mesh,
        in_specs=in_specs,
        out_specs=out_specs,
        check_vma=False,
    )
```

```python
import functools
import math

import jax
import jax.numpy as jnp
from jax import lax
from jax.experimental import pallas as pl
from jax.experimental.pallas import tpu as pltpu
from jax.sharding import PartitionSpec as P

L = 256
BINS = 128
TAPS = 64
HALF = 64
MAXOFF = 64

eps_time = 1e-05
eps_power = 1e-06
low_cut = 0.04
high_cut = 0.42

MESH = pl.DeviceIdType.MESH
F32 = jnp.float32
BF16 = jnp.bfloat16


def filter_taps(width, tap_count):
    lag_steps = jnp.arange(width, dtype=jnp.int32)[None, :]
    lag_value = lag_steps.astype(F32)
    centre = lag_value - (tap_count - 1) / 2.0
    hann_taper = 0.5 - 0.5 * jnp.cos(2.0 * math.pi * lag_value / (tap_count - 1))
    band_pass = 2.0 * high_cut * jnp.sinc(2.0 * high_cut * centre) - 2.0 * low_cut * jnp.sinc(
        2.0 * low_cut * centre
    )
    return jnp.where(lag_steps < tap_count, hann_taper * band_pass, F32(0.0))


def dft_rows(freq_bins, length, owners):
    positions = jnp.arange(length, dtype=jnp.int32)[None, :]
    angles = (positions * freq_bins[:, None] % length).astype(F32) * (2.0 * math.pi / length)
    table = jnp.stack([jnp.cos(angles), -jnp.sin(angles)]).astype(BF16)
    table = table.reshape(2, owners, -1, length)
    return jnp.swapaxes(table, 0, 1).reshape(-1, length)


def spectra(offsets, first_win, frames, fir, table, alive, frame, acc):
    wins = frames.shape[1]
    chans, seg_len = frames.shape[0], frames.shape[2]
    rows, batch = table.shape[0], min(8, wins)
    lanes = frame.shape[2]
    for t in range(seg_len // lanes):
        one = frames[:, :, t * lanes : (t + 1) * lanes].astype(F32)
        frame[t] = one.reshape(chans * wins, lanes)
    row = lax.broadcasted_iota(jnp.int32, (L, L), 0)
    column = lax.broadcasted_iota(jnp.int32, (L, L), 1)
    band = jnp.where(jnp.abs(row - column) <= HALF, F32(1), F32(0)).astype(BF16)
    spot = lax.broadcasted_iota(jnp.int32, (L, 1), 0)
    count = jnp.minimum(spot + HALF, L - 1) - jnp.maximum(spot - HALF, 0) + 1
    share = 1.0 / count.astype(F32)
    for base in range(0, wins, batch):
        shifted = []
        for w in range(base, base + batch):
            turn = lax.rem(seg_len - offsets[first_win + w], seg_len)
            one = jnp.concatenate(
                [frame[t, pl.ds(w, chans, stride=wins), :] for t in range(seg_len // lanes)], axis=1
            )
            shifted.append(pltpu.roll(one, turn, 1).astype(BF16))
        filtered = lax.dot_general(
            fir,
            jnp.concatenate(shifted, axis=0),
            (((1,), (1,)), ((), ())),
            preferred_element_type=F32,
        )
        size = jnp.abs(filtered)
        high = size.astype(BF16)
        rest = size - high.astype(F32)
        mid = rest.astype(BF16)
        low = (rest - mid.astype(F32)).astype(BF16)
        total = jnp.dot(band, high, preferred_element_type=F32)
        total += jnp.dot(band, mid, preferred_element_type=F32)
        total += jnp.dot(band, low, preferred_element_type=F32)
        normed = (filtered / (total * share + eps_time)).astype(BF16)
        bands = jnp.dot(table, normed, preferred_element_type=F32)
        for i in range(batch):
            acc[pl.ds(base + i, rows, stride=wins), :] = (
                bands[:, i * chans : (i + 1) * chans] * alive
            )


def gather_kernel(
    owners, sections, group,
    offsets, traces, taps, table, alive, gath,
    frames, frame, acc, spec, load_sem, put_sem,
    a2a_send, a2a_recv, up_send, up_recv, dn_send, dn_recv,
):
    chunks, _, wins, seg_len = frames.shape
    loads = [
        pltpu.make_async_copy(
            traces.at[:, pl.ds(j * wins, wins), :], frames.at[j], load_sem.at[j]
        )
        for j in range(chunks)
    ]
    for load in loads:
        load.start()
    chan = lax.axis_index("chan")
    place = lax.rem(chan, group)
    mine = lax.axis_index("freq") * sections + lax.axis_index("section")

    def other(d):
        q = mine
        for bit in range(d.bit_length()):
            if d >> bit & 1:
                q = q + (1 << bit) - 2 * (1 << bit) * lax.rem(mine // (1 << bit), 2)
        return q

    def peer(d):
        q = other(d)
        return {"freq": q // sections, "section": lax.rem(q, sections)}

    has_up, has_dn = place + 1 < group, place >= 1
    barrier = pltpu.get_barrier_semaphore()
    for d in range(1, owners):
        pl.semaphore_signal(barrier, inc=1, device_id=peer(d), device_id_type=MESH)

    @pl.when(has_up)
    def _():
        pl.semaphore_signal(barrier, inc=1, device_id={"chan": chan + 1}, device_id_type=MESH)

    @pl.when(has_dn)
    def _():
        pl.semaphore_signal(barrier, inc=1, device_id={"chan": chan - 1}, device_id_type=MESH)

    def a2a(d, j):
        return pltpu.make_async_remote_copy(
            src_ref=spec.at[j, other(d)],
            dst_ref=gath.at[place, mine, j],
            send_sem=a2a_send.at[d, j],
            recv_sem=a2a_recv.at[d, j],
            device_id=peer(d),
            device_id_type=MESH,
        )

    def own(j, up):
        return pltpu.make_async_remote_copy(
            src_ref=spec.at[j, mine],
            dst_ref=gath.at[place, mine, j],
            send_sem=(up_send if up else dn_send).at[0, 0, j],
            recv_sem=(up_recv if up else dn_recv).at[0, 0, j],
            device_id={"chan": chan + 1 if up else chan - 1},
            device_id_type=MESH,
        )

    def hop(k, d, up):
        block = place - k if up else place + k
        return pltpu.make_async_remote_copy(
            src_ref=gath.at[block, other(d)],
            dst_ref=gath.at[block, other(d)],
            send_sem=(up_send if up else dn_send).at[k, d, 0],
            recv_sem=(up_recv if up else dn_recv).at[k, d, 0],
            device_id={"chan": chan + 1 if up else chan - 1},
            device_id_type=MESH,
        )

    def arrival(k, d, j, up):
        block = place - k if up else place + k
        ref = gath.at[block, mine, j] if k == 1 and d == 0 else gath.at[block, other(d)]
        return pltpu.make_async_remote_copy(
            src_ref=ref,
            dst_ref=ref,
            send_sem=(up_send if up else dn_send).at[k - 1, d, j],
            recv_sem=(up_recv if up else dn_recv).at[k - 1, d, j],
            device_id={"chan": chan - 1 if up else chan + 1},
            device_id_type=MESH,
        )

    def put(j):
        return pltpu.make_async_copy(spec.at[j, mine], gath.at[place, mine, j], put_sem.at[j])

    ways = ((True, has_up), (False, has_dn))
    padded = jnp.broadcast_to(taps[...], (L, seg_len))
    fir = pltpu.roll(padded, 0, 1, stride=1, stride_axis=0).astype(BF16)
    lives = alive[...].astype(F32)
    for j in range(chunks):
        loads[j].wait()
        spectra(offsets, j * wins, frames[j], fir, table[...], lives, frame, acc)
        spec[j] = acc[...].astype(BF16).reshape(spec.shape[1:])
        if j == 0:
            pl.semaphore_wait(
                barrier, owners - 1 + has_up.astype(jnp.int32) + has_dn.astype(jnp.int32)
            )
        for up, goes in ways:

            @pl.when(goes)
            def _():
                own(j, up).start()

        for d in range(1, owners):
            a2a(d, j).start()
        put(j).start()
    for d in range(1, owners):
        for j in range(chunks):
            a2a(d, j).wait_recv()
        for up, goes in ways:

            @pl.when(goes)
            def _():
                hop(0, d, up).start()

    for k in range(1, group):
        for d in range(owners):
            for up, goes in ways:
                comes = place - k >= 0 if up else place + k < group

                @pl.when(comes)
                def _():
                    for j in range(chunks if k == 1 and d == 0 else 1):
                        arrival(k, d, j, up).wait_recv()

                @pl.when(comes & goes)
                def _():
                    hop(k, d, up).start()

    for j in range(chunks):
        put(j).wait()
        for d in range(1, owners):
            a2a(d, j).wait_send()
    for k in range(group - 1):
        for d in range(owners):
            for up, goes in ways:

                @pl.when((place - k >= 0 if up else place + k < group) & goes)
                def _():
                    if k == 0 and d == 0:
                        for j in range(chunks):
                            own(j, up).wait_send()
                    else:
                        hop(k, d, up).wait_send()


def cross_kernel(place, windows, data, out):
    group, owners, chunks, _, batch, wins, chans = data.shape
    mine = place[0]
    half = owners * chunks * wins
    for f in range(batch):

        def whitened(b):
            parts = [data[b, :, :, p, f].reshape(half, chans) for p in (0, 1)]
            values = jnp.concatenate(parts, axis=0).astype(F32)
            power = jnp.sum(values * values, axis=0, keepdims=True) * (1.0 / windows)
            return (values * lax.rsqrt(power + eps_power)).astype(BF16)

        right = jnp.concatenate([whitened(b) for b in range(group)], axis=1)
        own = whitened(mine)
        turned = jnp.concatenate([own[half:], -own[:half]], axis=0)
        left = jnp.concatenate([own, turned], axis=1)
        product = lax.dot_general(
            left, right, (((0,), (0,)), ((), ())), preferred_element_type=F32
        )
        scaled = (product * (1.0 / windows)).astype(BF16)
        out[0, f] = scaled[:chans]
        out[1, f] = scaled[chans:]


def local(sizes, traces, offsets, freq_bins, channel_alive):
    chans, wins, seg_len = traces.shape
    owners = sizes["freq"] * sizes["section"]
    group = min(8, sizes["chan"])
    bins = BINS // owners
    chunks = 2
    part = wins // chunks
    rows = 2 * bins * part
    dma = pltpu.SemaphoreType.DMA
    hbm = pl.BlockSpec(memory_space=pl.ANY)
    vmem = pl.BlockSpec(memory_space=pltpu.VMEM)
    gathered = pl.pallas_call(
        functools.partial(gather_kernel, owners, sizes["section"], group),
        in_specs=[pl.BlockSpec(memory_space=pltpu.SMEM), hbm, vmem, vmem, vmem],
        out_specs=hbm,
        out_shape=jax.ShapeDtypeStruct((group, owners, chunks, rows, chans), BF16),
        scratch_shapes=[
            pltpu.VMEM((chunks, chans, part, seg_len), BF16),
            pltpu.VMEM((seg_len // 128, chans * part, 128), F32),
            pltpu.VMEM((2 * BINS * part, chans), F32),
            pltpu.VMEM((chunks, owners, rows, chans), BF16),
            dma((chunks,)),
            dma((chunks,)),
        ]
        + [dma((owners, chunks))] * 2
        + [dma((group, owners, chunks))] * 4,
        compiler_params=pltpu.CompilerParams(collective_id=0, has_side_effects=True),
        name="gather",
    )(
        offsets,
        traces,
        filter_taps(seg_len, TAPS),
        dft_rows(freq_bins, L, owners),
        channel_alive.reshape(1, chans),
    )
    fold = 8
    place = lax.rem(lax.axis_index("chan"), group).astype(jnp.int32).reshape(1)
    return pl.pallas_call(
        lambda place, data, out: cross_kernel(place, wins * owners, data, out),
        grid_spec=pltpu.PrefetchScalarGridSpec(
            num_scalar_prefetch=1,
            grid=(bins // fold,),
            in_specs=[
                pl.BlockSpec(
                    (group, owners, chunks, 2, fold, part, chans),
                    lambda i, _: (0, 0, 0, 0, i, 0, 0),
                )
            ],
            out_specs=pl.BlockSpec((2, fold, chans, group * chans), lambda i, _: (0, i, 0, 0)),
        ),
        out_shape=jax.ShapeDtypeStruct((2, bins, chans, group * chans), BF16),
        name="cross",
    )(place, gathered.reshape(group, owners, chunks, 2, bins, part, chans))


def solution(mesh):
    in_specs = (
        P(("grp", "chan"), ("freq", "section"), None),
        P(("grp", "freq", "section")),
        P(),
        P(("grp", "chan")),
    )
    out_specs = P(None, ("freq", "section"), ("grp", "chan"), None)
    sizes = dict(mesh.shape)
    return jax.shard_map(
        functools.partial(local, sizes),
        mesh=mesh,
        in_specs=in_specs,
        out_specs=out_specs,
        check_vma=False,
    )
```

```python
import functools
import math

import jax
import jax.numpy as jnp
from jax import lax
from jax.experimental import pallas as pl
from jax.experimental.pallas import tpu as pltpu
from jax.sharding import PartitionSpec as P

L = 256
BINS = 128
TAPS = 64
HALF = 64
MAXOFF = 64

eps_time = 1e-05
eps_power = 1e-06
low_cut = 0.04
high_cut = 0.42

MESH = pl.DeviceIdType.MESH
F32 = jnp.float32
BF16 = jnp.bfloat16


def filter_taps(width, tap_count):
    lag_steps = jnp.arange(width, dtype=jnp.int32)[None, :]
    lag_value = lag_steps.astype(F32)
    centre = lag_value - (tap_count - 1) / 2.0
    hann_taper = 0.5 - 0.5 * jnp.cos(2.0 * math.pi * lag_value / (tap_count - 1))
    band_pass = 2.0 * high_cut * jnp.sinc(2.0 * high_cut * centre) - 2.0 * low_cut * jnp.sinc(
        2.0 * low_cut * centre
    )
    return jnp.where(lag_steps < tap_count, hann_taper * band_pass, F32(0.0))


def dft_rows(freq_bins, length, owners):
    positions = jnp.arange(length, dtype=jnp.int32)[None, :]
    angles = (positions * freq_bins[:, None] % length).astype(F32) * (2.0 * math.pi / length)
    table = jnp.stack([jnp.cos(angles), -jnp.sin(angles)]).astype(BF16)
    table = table.reshape(2, owners, -1, length)
    return jnp.swapaxes(table, 0, 1).reshape(-1, length)


def spectra(offsets, first_win, frames, fir, table, alive, frame, acc):
    wins = frames.shape[1]
    chans, seg_len = frames.shape[0], frames.shape[2]
    rows, batch = table.shape[0], min(8, wins)
    lanes = frame.shape[2]
    for t in range(seg_len // lanes):
        one = frames[:, :, t * lanes : (t + 1) * lanes].astype(F32)
        frame[t] = one.reshape(chans * wins, lanes)
    row = lax.broadcasted_iota(jnp.int32, (L, L), 0)
    column = lax.broadcasted_iota(jnp.int32, (L, L), 1)
    band = jnp.where(jnp.abs(row - column) <= HALF, F32(1), F32(0)).astype(BF16)
    spot = lax.broadcasted_iota(jnp.int32, (L, 1), 0)
    count = jnp.minimum(spot + HALF, L - 1) - jnp.maximum(spot - HALF, 0) + 1
    share = 1.0 / count.astype(F32)
    for base in range(0, wins, batch):
        shifted = []
        for w in range(base, base + batch):
            turn = lax.rem(seg_len - offsets[first_win + w], seg_len)
            one = jnp.concatenate(
                [frame[t, pl.ds(w, chans, stride=wins), :] for t in range(seg_len // lanes)], axis=1
            )
            shifted.append(pltpu.roll(one, turn, 1).astype(BF16))
        filtered = lax.dot_general(
            fir,
            jnp.concatenate(shifted, axis=0),
            (((1,), (1,)), ((), ())),
            preferred_element_type=F32,
        )
        size = jnp.abs(filtered)
        high = size.astype(BF16)
        rest = size - high.astype(F32)
        mid = rest.astype(BF16)
        low = (rest - mid.astype(F32)).astype(BF16)
        total = jnp.dot(band, high, preferred_element_type=F32)
        total += jnp.dot(band, mid, preferred_element_type=F32)
        total += jnp.dot(band, low, preferred_element_type=F32)
        normed = (filtered / (total * share + eps_time)).astype(BF16)
        bands = jnp.dot(table, normed, preferred_element_type=F32)
        for i in range(batch):
            acc[pl.ds(base + i, rows, stride=wins), :] = (
                bands[:, i * chans : (i + 1) * chans] * alive
            )


def gather_kernel(
    owners, sections, group,
    offsets, traces, taps, table, alive, gath,
    frames, frame, acc, spec, load_sem, put_sem,
    a2a_send, a2a_recv, up_send, up_recv, dn_send, dn_recv,
):
    chunks, _, wins, seg_len = frames.shape
    loads = [
        pltpu.make_async_copy(
            traces.at[:, pl.ds(j * wins, wins), :], frames.at[j], load_sem.at[j]
        )
        for j in range(chunks)
    ]
    for load in loads:
        load.start()
    chan = lax.axis_index("chan")
    place = lax.rem(chan, group)
    mine = lax.axis_index("freq") * sections + lax.axis_index("section")

    def other(d):
        q = mine
        for bit in range(d.bit_length()):
            if d >> bit & 1:
                q = q + (1 << bit) - 2 * (1 << bit) * lax.rem(mine // (1 << bit), 2)
        return q

    def peer(d):
        q = other(d)
        return {"freq": q // sections, "section": lax.rem(q, sections)}

    has_up, has_dn = place + 1 < group, place >= 1
    barrier = pltpu.get_barrier_semaphore()
    for d in range(1, owners):
        pl.semaphore_signal(barrier, inc=1, device_id=peer(d), device_id_type=MESH)

    @pl.when(has_up)
    def _():
        pl.semaphore_signal(barrier, inc=1, device_id={"chan": chan + 1}, device_id_type=MESH)

    @pl.when(has_dn)
    def _():
        pl.semaphore_signal(barrier, inc=1, device_id={"chan": chan - 1}, device_id_type=MESH)

    def a2a(d, j):
        return pltpu.make_async_remote_copy(
            src_ref=spec.at[j, other(d)],
            dst_ref=gath.at[place, mine, j],
            send_sem=a2a_send.at[d, j],
            recv_sem=a2a_recv.at[d, j],
            device_id=peer(d),
            device_id_type=MESH,
        )

    def own(j, up):
        return pltpu.make_async_remote_copy(
            src_ref=spec.at[j, mine],
            dst_ref=gath.at[place, mine, j],
            send_sem=(up_send if up else dn_send).at[0, 0, j],
            recv_sem=(up_recv if up else dn_recv).at[0, 0, j],
            device_id={"chan": chan + 1 if up else chan - 1},
            device_id_type=MESH,
        )

    def hop(k, d, up):
        block = place - k if up else place + k
        return pltpu.make_async_remote_copy(
            src_ref=gath.at[block, other(d)],
            dst_ref=gath.at[block, other(d)],
            send_sem=(up_send if up else dn_send).at[k, d, 0],
            recv_sem=(up_recv if up else dn_recv).at[k, d, 0],
            device_id={"chan": chan + 1 if up else chan - 1},
            device_id_type=MESH,
        )

    def arrival(k, d, j, up):
        block = place - k if up else place + k
        ref = gath.at[block, mine, j] if k == 1 and d == 0 else gath.at[block, other(d)]
        return pltpu.make_async_remote_copy(
            src_ref=ref,
            dst_ref=ref,
            send_sem=(up_send if up else dn_send).at[k - 1, d, j],
            recv_sem=(up_recv if up else dn_recv).at[k - 1, d, j],
            device_id={"chan": chan - 1 if up else chan + 1},
            device_id_type=MESH,
        )

    def put(j):
        return pltpu.make_async_copy(spec.at[j, mine], gath.at[place, mine, j], put_sem.at[j])

    ways = ((True, has_up), (False, has_dn))
    padded = jnp.broadcast_to(taps[...], (L, seg_len))
    fir = pltpu.roll(padded, 0, 1, stride=1, stride_axis=0).astype(BF16)
    lives = alive[...].astype(F32)
    for j in range(chunks):
        loads[j].wait()
        spectra(offsets, j * wins, frames[j], fir, table[...], lives, frame, acc)
        spec[j] = acc[...].astype(BF16).reshape(spec.shape[1:])
        if j == 0:
            pl.semaphore_wait(
                barrier, owners - 1 + has_up.astype(jnp.int32) + has_dn.astype(jnp.int32)
            )
        for up, goes in ways:

            @pl.when(goes)
            def _():
                own(j, up).start()

        for d in range(1, owners):
            a2a(d, j).start()
        put(j).start()
    for d in range(1, owners):
        for j in range(chunks):
            a2a(d, j).wait_recv()
        for up, goes in ways:

            @pl.when(goes)
            def _():
                hop(0, d, up).start()

    for k in range(1, group):
        for d in range(owners):
            for up, goes in ways:
                comes = place - k >= 0 if up else place + k < group

                @pl.when(comes)
                def _():
                    for j in range(chunks if k == 1 and d == 0 else 1):
                        arrival(k, d, j, up).wait_recv()

                @pl.when(comes & goes)
                def _():
                    hop(k, d, up).start()

    for j in range(chunks):
        put(j).wait()
        for d in range(1, owners):
            a2a(d, j).wait_send()
    for k in range(group - 1):
        for d in range(owners):
            for up, goes in ways:

                @pl.when((place - k >= 0 if up else place + k < group) & goes)
                def _():
                    if k == 0 and d == 0:
                        for j in range(chunks):
                            own(j, up).wait_send()
                    else:
                        hop(k, d, up).wait_send()


def cross_kernel(place, windows, data, out, held):
    group, owners, chunks, _, batch, wins, chans = data.shape
    mine = place[0]
    half = owners * chunks * wins
    for f in range(batch):

        def whitened(b):
            parts = [data[b, :, :, p, f].reshape(half, chans) for p in (0, 1)]
            values = jnp.concatenate(parts, axis=0).astype(F32)
            power = jnp.sum(values * values, axis=0, keepdims=True) * (1.0 / windows)
            return (values * lax.rsqrt(power + eps_power)).astype(BF16)

        blocks = [whitened(b) for b in range(group)]
        right = jnp.concatenate(blocks, axis=1)
        for b in range(group):
            held[f, b] = blocks[b]
        own = held[f, mine]
        turned = jnp.concatenate([own[half:], -own[:half]], axis=0)
        left = jnp.concatenate([own, turned], axis=1)
        product = lax.dot_general(
            left, right, (((0,), (0,)), ((), ())), preferred_element_type=F32
        )
        scaled = (product * (1.0 / windows)).astype(BF16)
        out[0, f] = scaled[:chans]
        out[1, f] = scaled[chans:]


def local(sizes, traces, offsets, freq_bins, channel_alive):
    chans, wins, seg_len = traces.shape
    owners = sizes["freq"] * sizes["section"]
    group = min(8, sizes["chan"])
    bins = BINS // owners
    chunks = 2
    part = wins // chunks
    rows = 2 * bins * part
    dma = pltpu.SemaphoreType.DMA
    hbm = pl.BlockSpec(memory_space=pl.ANY)
    vmem = pl.BlockSpec(memory_space=pltpu.VMEM)
    gathered = pl.pallas_call(
        functools.partial(gather_kernel, owners, sizes["section"], group),
        in_specs=[pl.BlockSpec(memory_space=pltpu.SMEM), hbm, vmem, vmem, vmem],
        out_specs=hbm,
        out_shape=jax.ShapeDtypeStruct((group, owners, chunks, rows, chans), BF16),
        scratch_shapes=[
            pltpu.VMEM((chunks, chans, part, seg_len), BF16),
            pltpu.VMEM((seg_len // 128, chans * part, 128), F32),
            pltpu.VMEM((2 * BINS * part, chans), F32),
            pltpu.VMEM((chunks, owners, rows, chans), BF16),
            dma((chunks,)),
            dma((chunks,)),
        ]
        + [dma((owners, chunks))] * 2
        + [dma((group, owners, chunks))] * 4,
        compiler_params=pltpu.CompilerParams(collective_id=0, has_side_effects=True),
        name="gather",
    )(
        offsets,
        traces,
        filter_taps(seg_len, TAPS),
        dft_rows(freq_bins, L, owners),
        channel_alive.reshape(1, chans),
    )
    fold = 8
    place = lax.rem(lax.axis_index("chan"), group).astype(jnp.int32).reshape(1)
    return pl.pallas_call(
        lambda place, *refs: cross_kernel(place, wins * owners, *refs),
        grid_spec=pltpu.PrefetchScalarGridSpec(
            num_scalar_prefetch=1,
            grid=(bins // fold,),
            in_specs=[
                pl.BlockSpec(
                    (group, owners, chunks, 2, fold, part, chans),
                    lambda i, _: (0, 0, 0, 0, i, 0, 0),
                )
            ],
            out_specs=pl.BlockSpec((2, fold, chans, group * chans), lambda i, _: (0, i, 0, 0)),
            scratch_shapes=[pltpu.VMEM((fold, group, 2 * owners * wins, chans), BF16)],
        ),
        out_shape=jax.ShapeDtypeStruct((2, bins, chans, group * chans), BF16),
        name="cross",
    )(place, gathered.reshape(group, owners, chunks, 2, bins, part, chans))


def solution(mesh):
    in_specs = (
        P(("grp", "chan"), ("freq", "section"), None),
        P(("grp", "freq", "section")),
        P(),
        P(("grp", "chan")),
    )
    out_specs = P(None, ("freq", "section"), ("grp", "chan"), None)
    sizes = dict(mesh.shape)
    return jax.shard_map(
        functools.partial(local, sizes),
        mesh=mesh,
        in_specs=in_specs,
        out_specs=out_specs,
        check_vma=False,
    )
```
